256 devices in a mesh: rollout: 8 (over z), branch: 8 (over y_lo, x), tensor: 4 (over y_hi, core).
Axes of the slice: x: 4, y: 4 (y_hi: 2, y_lo: 2; y = y_hi * 2 + y_lo), z: 8, core: 2. Of those that a mesh axis runs over, the one named last changes fastest.
Arguments:
- tokens: bfloat16 [32768, 2048], P(('rollout', 'branch')), parts along dimension 0, as said below
- parents: int32 [128], P('rollout'), parts along dimension 0, may hold values from 0 to 14, as said below
- lengths: int32 [128], P('rollout'), parts along dimension 0, may hold values from 128 to 256, as said below
- lin_qkv: bfloat16 [2048, 3, 1024], P(None, None, 'tensor'), may hold values from -0.125 to 0.125
- lin_gates: bfloat16 [2048, 2, 8], P(None, None, 'tensor'), as said below
- decay_rate: float32 [8], P('tensor'), as said below
- lin_out: bfloat16 [1024, 2048], P('tensor'), may hold values from -4 to 4
- norm_gain: float32 [2048], replicated, may hold values from 0.1 to 1.9
- att_q: bfloat16 [2048, 2048], P(None, 'tensor'), as said below
- att_kv: bfloat16 [2048, 2, 512], replicated, as said below
Outputs:
- lin_mixed: bfloat16 [32768, 2048], P(('rollout', 'branch', 'tensor')), parts along dimension 0
- att_out: bfloat16 [32768, 2048], P(('rollout', 'branch'), 'tensor'), parts along dimension 0
The draws below stay inside these ranges and needn't reach their ends.
There are 8 independent parts, one for each index of `rollout`. The reference program is written for one: setup_inputs(seed, part) draws one part's arguments, and reference() takes and returns one part's arrays. A program takes and returns all parts, laid end to end along the dimension named above; an argument that names none is the same for every part. Nothing has to cross between parts.
Inputs may be any that keep to these rules, and one draw needn't show every extreme that they name: parents[0] = 0 marks the root; every other branch's parent is an earlier branch; the last branch's parent is the branch just before it. `lengths`: a multiple of 128; some branch has 256 valid tokens and some has 128. `decay_rate`: positive. `tokens`: entries of order one. `lin_gates`: entries of order one over the square root of 2048. `att_q`: entries of order one over the square root of 2048. `att_kv`: entries of order one over the square root of 2048.
All inputs are finite; a program needn't handle non-finite values.
Results may differ from the reference program's by a relative error of at most 0.035.
Values may be sent and summed in bfloat16 or wider, within the bound.
No kernel may reach another device: no remote copies, remote signals or barrier semaphores. Data moves between devices by JAX's collectives and lax.ppermute only.
A program may use at most 128 MiB of HBM per device.

```python
import math
import jax
import jax.numpy as jnp
from jax import lax

D = 2048
LIN_HEADS = 8
LIN_DIM = 128
Q_HEADS = 8
KV_HEADS = 2
ATT_DIM = 256
BLOCK = 64
TILE = 128
SEG = 256
SEGMENTS = 16
ROWS = 4096


token_shift = 0.5


write_bias = 2.2


def draw_parents(key, part):
    spine_key = jax.random.fold_in(key, 1)
    pick_key = jax.random.fold_in(key, 2)
    seg_ids = jnp.arange(SEGMENTS, dtype=jnp.int32)
    on_spine = (jax.random.randint(spine_key, (SEGMENTS,), 0, 4) < 3) | (seg_ids == 0) | (seg_ids >= SEGMENTS - 2)
    marks = jnp.where(on_spine, seg_ids, 0).astype(jnp.int32)
    latest = lax.cummax(marks, axis=0)
    previous = jnp.concatenate([jnp.zeros((1,), jnp.int32), latest[:-1].astype(jnp.int32)])
    upper = jnp.maximum(seg_ids, 1)
    chosen = jax.random.randint(pick_key, (SEGMENTS,), 0, upper).astype(jnp.int32)
    result = jnp.where(on_spine, previous, chosen)
    return jnp.where(seg_ids == 0, 0, result).astype(jnp.int32)


def draw_lengths(key, part):
    first_key = jax.random.fold_in(key, 11)
    second_key = jax.random.fold_in(key, 12)
    third_key = jax.random.fold_in(key, 13)
    seg_ids = jnp.arange(SEGMENTS)
    tiles = jax.random.randint(first_key, (SEGMENTS,), 1, SEG // TILE + 1) * TILE
    longest = jax.random.randint(second_key, (), 0, SEGMENTS)
    shortest = (longest + 1 + jax.random.randint(third_key, (), 0, SEGMENTS - 1)) % SEGMENTS
    chosen = jnp.where(seg_ids == longest, SEG, jnp.where(seg_ids == shortest, TILE, tiles))
    return chosen.astype(jnp.int32)


def draw_decay_rate(key, part):
    pick_key = jax.random.fold_in(key, 21)
    slow_key = jax.random.fold_in(key, 22)
    fast_key = jax.random.fold_in(key, 23)
    share = 0.5
    is_slow = jax.random.uniform(pick_key, (LIN_HEADS,), jnp.float32) < share
    slow_log = jax.random.uniform(slow_key, (LIN_HEADS,), jnp.float32, math.log(0.1), math.log(2.0))
    fast_log = jax.random.uniform(fast_key, (LIN_HEADS,), jnp.float32, math.log(0.02), math.log(0.06))
    slow_rate = jnp.exp(slow_log) / ROWS
    fast_rate = jnp.exp(fast_log)
    return jnp.where(is_slow, slow_rate, fast_rate).astype(jnp.float32)


def weight_noise(key, shape, fan_in):
    raw = jax.random.truncated_normal(key, -6.0, 6.0, shape, jnp.float32)
    return raw / math.sqrt(fan_in)


def draw_tokens(key, part):
    noise_key = jax.random.fold_in(key, 61)
    raw = jax.random.truncated_normal(noise_key, -6.0, 6.0, (ROWS, D), jnp.float32)
    return (raw + token_shift).astype(jnp.bfloat16)


def draw_lin_gates(key, part):
    noise = weight_noise(jax.random.fold_in(key, 51), (D, 2, LIN_HEADS), D)
    write_column = (jnp.arange(2) == 1).astype(jnp.float32)
    shift = write_bias / (token_shift * D)
    result = noise - shift * write_column[None, :, None]
    return result.astype(jnp.bfloat16)


def draw_att_q(key, part):
    result = weight_noise(jax.random.fold_in(key, 41), (D, Q_HEADS * ATT_DIM), D)
    return result.astype(jnp.bfloat16)


def draw_att_kv(key, part):
    result = weight_noise(jax.random.fold_in(key, 42), (D, 2, KV_HEADS * ATT_DIM), D)
    return result.astype(jnp.bfloat16)


def shard_levels(rng, extent, cuts, least, high):
    gain = 1.0
    for dim, parts in cuts:
        draws = jax.random.uniform(jax.random.fold_in(jax.random.fold_in(rng, 6), dim), (parts,), jnp.float32, least / len(cuts), high / len(cuts))
        gain = gain * jnp.repeat(jnp.exp(draws), extent[dim] // parts).reshape((-1,) + (1,) * (len(extent) - 1 - dim))
    return gain


def gaussian(rng, shape, scale, most, cuts=(), kind=jnp.bfloat16):
    loudness = shard_levels(rng, shape, cuts, -0.22, 0.18) if cuts else 1.0
    entries = jax.random.normal(rng, shape, jnp.float32) * scale * loudness
    return jnp.minimum(jnp.maximum(entries, -most), most).astype(kind)


def setup_inputs(seed: int = 0, part: int = 0) -> dict:
    key_of = jax.random.split(jax.random.key(seed), 11)
    part_keys = jax.random.split(jax.random.fold_in(key_of[10], part), 11)
    return {
        "tokens": draw_tokens(jax.random.fold_in(jax.random.fold_in(key_of[10], part), 71), part),
        "parents": draw_parents(jax.random.fold_in(jax.random.fold_in(key_of[10], part), 71), part),
        "lengths": draw_lengths(jax.random.fold_in(jax.random.fold_in(key_of[10], part), 71), part),
        "lin_qkv": gaussian(key_of[3], (D, 3, LIN_HEADS * LIN_DIM), D ** -0.5, 0.125, ((2, 4),)),
        "lin_gates": draw_lin_gates(jax.random.fold_in(key_of[10], 71), part),
        "decay_rate": draw_decay_rate(jax.random.fold_in(key_of[10], 71), part),
        "lin_out": gaussian(key_of[6], (LIN_HEADS * LIN_DIM, D), 2 ** -0.5, 4.0, ((0, 4),)),
        "norm_gain": jnp.clip(1.0 + 0.18 * jax.random.normal(key_of[7], (D,), jnp.float32), 0.1, 1.9),
        "att_q": draw_att_q(jax.random.fold_in(key_of[10], 71), part),
        "att_kv": draw_att_kv(jax.random.fold_in(key_of[10], 71), part),
    }


highest = lax.Precision.HIGHEST

def unit_rows(matrix):
    return matrix * lax.rsqrt(lax.optimization_barrier(jnp.sum(matrix * matrix, axis=-1, keepdims=True)) + 1e-06)

def ancestor_table(parent_map):
    count = parent_map.shape[0]

    def widen(counter, table):
        return parent_map + jnp.dot(parent_map, table, precision=highest)
    return lax.fori_loop(0, count - 1, widen, parent_map)

def block_terms(q_unit, k_unit, values, beta, log_decay):
    blocks = q_unit.shape[0] // BLOCK

    def split_block(array):
        shaped = array.reshape((blocks, BLOCK) + array.shape[1:])
        return jnp.swapaxes(shaped, 1, 2)
    queries = split_block(q_unit)
    keys_blk = split_block(k_unit)
    vals_blk = split_block(values)
    beta_blk = split_block(beta)
    decay_blk = jnp.cumsum(split_block(log_decay), axis=-1)
    final_decay = decay_blk[..., -1:]
    gap = decay_blk[..., :, None] - decay_blk[..., None, :]
    places = jnp.arange(BLOCK)
    strict = places[:, None] > places[None, :]
    inclusive = places[:, None] >= places[None, :]
    key_key = jnp.einsum('nhtd,nhsd->nhts', keys_blk, keys_blk, precision=highest)
    query_key = jnp.einsum('nhtd,nhsd->nhts', queries, keys_blk, precision=highest)
    lower_part = jnp.where(strict, beta_blk[..., :, None] * jnp.exp(jnp.where(strict, gap, 0.0)) * key_key, 0.0)
    system = lower_part + jnp.eye(BLOCK, dtype=lower_part.dtype)
    right_hand = jnp.concatenate([beta_blk[..., None] * vals_blk, (beta_blk * jnp.exp(decay_blk))[..., None] * keys_blk], axis=-1)
    solved = jax.scipy.linalg.solve_triangular(system, right_hand, lower=True, unit_diagonal=True)
    value_width = vals_blk.shape[-1]
    pseudo = solved[..., :value_width]
    weighted = solved[..., value_width:]
    carried_keys = jnp.exp(final_decay - decay_blk)[..., None] * keys_blk
    scaled_queries = jnp.exp(decay_blk)[..., None] * queries
    mixing = jnp.where(inclusive, jnp.exp(jnp.where(inclusive, gap, 0.0)) * query_key, 0.0)
    overall = jnp.exp(final_decay[..., 0])
    return (pseudo, weighted, carried_keys, scaled_queries, mixing, overall)

def run_outputs(initial, terms):

    def advance(current, block_part):
        pseudo, weighted, carried_keys, scaled_queries, mixing, overall = block_part
        update = pseudo - jnp.einsum('htk,hkm->htm', weighted, current, precision=highest)
        produced = jnp.einsum('htk,hkm->htm', scaled_queries, current, precision=highest)
        produced = produced + jnp.einsum('hts,hsm->htm', mixing, update, precision=highest)
        renewed = overall[:, None, None] * current + jnp.einsum('htk,htm->hkm', carried_keys, update, precision=highest)
        return (renewed, produced)
    final_state, produced = lax.scan(advance, initial, terms)
    blocks, head_count, block_len, value_width = produced.shape
    return (final_state, jnp.swapaxes(produced, 1, 2).reshape(blocks * block_len, head_count, value_width))

def reference(tokens, parents, lengths, lin_qkv, lin_gates, decay_rate, lin_out, norm_gain, att_q, att_kv):
    seg_ids = jnp.arange(SEGMENTS)
    parent_map = ((parents[:, None] == seg_ids[None, :]) & (seg_ids[:, None] > 0)).astype(jnp.float32)
    ancestors = (ancestor_table(parent_map) > 0.5).astype(jnp.int32)
    row_ids = jnp.arange(ROWS)
    row_seg = row_ids // SEG
    positions = row_ids % SEG
    row_limit = lax.optimization_barrier(jnp.sum(jnp.where(row_seg[:, None] == seg_ids[None, :], lengths[None, :], 0), axis=1))
    valid = positions < row_limit
    projected = jnp.dot(tokens.astype(jnp.float32), lin_qkv.reshape(D, -1).astype(jnp.float32), preferred_element_type=jnp.float32)
    projected = projected.reshape(ROWS, 3, LIN_HEADS, LIN_DIM)
    q_unit = unit_rows(projected[:, 0]) / math.sqrt(LIN_DIM)
    k_unit = unit_rows(projected[:, 1])
    values = projected[:, 2]
    gate_raw = jnp.dot(tokens.astype(jnp.float32), lin_gates.reshape(D, -1).astype(jnp.float32), preferred_element_type=jnp.float32).reshape(ROWS, 2, LIN_HEADS)
    beta = jnp.where(valid[:, None], jax.nn.sigmoid(gate_raw[:, 1]), 0.0)
    log_decay = jnp.where(valid[:, None], -decay_rate[None, :] * jax.nn.softplus(gate_raw[:, 0]), 0.0)
    ends = jnp.zeros((SEGMENTS, LIN_HEADS, LIN_DIM, LIN_DIM), jnp.float32)
    pieces = []
    for segment in range(SEGMENTS):
        lower_row = segment * SEG
        upper_row = lower_row + SEG
        terms = block_terms(q_unit[lower_row:upper_row], k_unit[lower_row:upper_row], values[lower_row:upper_row], beta[lower_row:upper_row], log_decay[lower_row:upper_row])
        if segment == 0:
            initial = jnp.zeros((LIN_HEADS, LIN_DIM, LIN_DIM), jnp.float32)
        else:
            initial = lax.dynamic_index_in_dim(ends, parents[segment], 0, keepdims=False)
        final_state, produced = run_outputs(initial, terms)
        ends = ends.at[segment].set(final_state)
        pieces.append(produced)
    lin_heads = jnp.concatenate(pieces, axis=0)
    lin_values = jnp.where(valid[:, None], lin_heads.reshape(ROWS, -1), 0.0).astype(jnp.bfloat16)
    mixed_sum = tokens.astype(jnp.float32) + jnp.dot(lin_values.astype(jnp.float32), lin_out.astype(jnp.float32), preferred_element_type=jnp.float32)
    lin_mixed = mixed_sum.astype(jnp.bfloat16)
    normed = (mixed_sum * lax.rsqrt(lax.optimization_barrier(jnp.mean(mixed_sum * mixed_sum, axis=-1, keepdims=True)) + 1e-06) * norm_gain).astype(jnp.bfloat16)
    att_queries = jnp.dot(normed.astype(jnp.float32), att_q.astype(jnp.float32), preferred_element_type=jnp.float32).astype(jnp.bfloat16)
    att_kvs = jnp.dot(normed.astype(jnp.float32), att_kv.reshape(D, -1).astype(jnp.float32), preferred_element_type=jnp.float32).astype(jnp.bfloat16)
    att_kvs = att_kvs.reshape(ROWS, 2, KV_HEADS, ATT_DIM)
    key_full = att_kvs[:, 0].astype(jnp.float32)
    value_full = att_kvs[:, 1].astype(jnp.float32)
    group = Q_HEADS // KV_HEADS
    key_valid = valid
    local_pos = jnp.arange(SEG)
    outputs = []
    for segment in range(SEGMENTS):
        lower_row = segment * SEG
        query_block = att_queries[lower_row:lower_row + SEG].astype(jnp.float32).reshape(SEG, KV_HEADS, group, ATT_DIM)
        scores = jnp.einsum('qcgd,kcd->cgqk', query_block, key_full, precision=highest) / math.sqrt(ATT_DIM)
        is_ancestor = ancestors[segment][row_seg] > 0
        own_branch = (row_seg == segment)[None, :] & (positions[None, :] <= local_pos[:, None])
        allowed = key_valid[None, :] & (is_ancestor[None, :] | own_branch)
        masked = jnp.where(allowed[None, None], scores, -1e+30)
        top = lax.optimization_barrier(jnp.max(masked, axis=-1, keepdims=True))
        numer = jnp.where(allowed[None, None], jnp.exp(scores - top), 0.0)
        denominators = lax.optimization_barrier(jnp.sum(numer, axis=-1))
        weights = numer.astype(jnp.bfloat16)
        weights = lax.optimization_barrier(weights).astype(jnp.float32)
        summed = jnp.einsum('cgqk,kcd->cgqd', weights, value_full, precision=highest)
        result = summed / denominators[..., None]
        result = jnp.transpose(result, (2, 0, 1, 3)).reshape(SEG, Q_HEADS * ATT_DIM)
        query_valid = valid[lower_row:lower_row + SEG]
        outputs.append(jnp.where(query_valid[:, None], result, 0.0).astype(jnp.bfloat16))
    att_out = jnp.concatenate(outputs, axis=0)
    return (lin_mixed, att_out)
```

```python
import math

import jax
import jax.numpy as jnp
from jax import lax
from jax.experimental import pallas as pl
from jax.experimental.pallas import tpu as pltpu
from jax.sharding import PartitionSpec as P

KV_HEADS = 2
ATT_DIM = 256
SEG = 256
HALF = 128
HEAD = 128
LOCAL = 2
HEADS = 2
PACK = 144
ROW = 4
TILES = 4
NEG = -1e30

f32 = jnp.float32
bf16 = jnp.bfloat16


def halves(x):
    high = x.astype(bf16)
    return high, (x - high.astype(f32)).astype(bf16)


def mm(a, b):
    return jnp.dot(a, b, preferred_element_type=f32)


def mm_t(a, b):
    return lax.dot_general(a, b, (((1,), (1,)), ((), ())), preferred_element_type=f32)


def dot3(a, b):
    ah, al = halves(a)
    bh, bl = halves(b)
    return mm(ah, bh) + (mm(ah, bl) + mm(al, bh))


def dot3_packed(a, b):
    ah, al = halves(a)
    bh, bl = halves(b)
    return mm(jnp.concatenate([ah, al], 1), jnp.concatenate([bh, bh], 0)) + mm(ah, bl)


def dot3_t(a, b):
    ah, al = halves(a)
    bh, bl = halves(b)
    return mm_t(ah, bh) + (mm_t(ah, bl) + mm_t(al, bh))


def running_sum(x):
    rows = lax.broadcasted_iota(jnp.int32, x.shape, 0)
    step = 1
    while step < x.shape[0]:
        x = x + jnp.where(rows >= step, pltpu.roll(x, step, 0), 0.0)
        step *= 2
    return x


def wide(a, b):
    high, low = halves(a)
    return mm(jnp.concatenate([high, low], 1), jnp.concatenate([b, b], 0))


def maps_kernel(len_ref, rate_ref, gate_in, tok_hbm, w_hbm, packet_ref, k_ref, x_ref, d_ref,
                tok_ref, w_ref, gate_ref, sems):
    branch = lax.axis_index("branch")
    width = HEADS * HEAD
    pairs = [(j, h) for j in range(LOCAL) for h in range(HEADS)]
    loads = [
        pltpu.make_async_copy(w_hbm.at[1], w_ref.at[0], sems.at[0]),
        pltpu.make_async_copy(tok_hbm.at[pl.ds(0, SEG)], tok_ref.at[0], sems.at[1]),
        pltpu.make_async_copy(tok_hbm.at[pl.ds(SEG, SEG)], tok_ref.at[1], sems.at[2]),
        pltpu.make_async_copy(w_hbm.at[2], w_ref.at[1], sems.at[3]),
    ]
    for load in loads:
        load.start()
    gate_ref[...] = jnp.zeros(gate_ref.shape, bf16)
    for c in range(2):
        gate_ref[c * HEADS : (c + 1) * HEADS, :] = gate_in[c]
    lane = lax.broadcasted_iota(jnp.int32, (1, 16), 1)
    rate = jnp.where(lane == 0, rate_ref[0], jnp.where(lane == 1, rate_ref[1], 0.0))
    row = lax.broadcasted_iota(jnp.int32, (SEG, SEG), 0)
    col = lax.broadcasted_iota(jnp.int32, (SEG, SEG), 1)
    gate_row = lax.broadcasted_iota(jnp.int32, (SEG, 16), 0)
    pack_row = lax.broadcasted_iota(jnp.int32, (PACK - HEAD, SEG), 0)
    strict = row > col
    differ = row[:HALF, :HALF] ^ col[:HALF, :HALF]
    loads[0].wait()
    keys, decays, betas = [], [], []
    for j in range(LOCAL):
        loads[1 + j].wait()
        keys.append(mm(tok_ref[j], w_ref[0]))
        gates = mm_t(tok_ref[j], gate_ref[...])
        valid = gate_row < len_ref[branch * LOCAL + j]
        betas.append(jnp.where(valid, 1.0 / (1.0 + jnp.exp(-gates)), 0.0))
        soft = jnp.maximum(gates, 0.0) + jnp.log1p(jnp.exp(-jnp.abs(gates)))
        decays.append(running_sum(jnp.where(valid, -rate * soft, 0.0)))
        d_ref[j * SEG : (j + 1) * SEG, :] = decays[j]
    loads[3].wait()
    unit, lowers, rights, blocks = [], [], [], []
    for j, h in pairs:
        key = keys[j][:, h * HEAD : (h + 1) * HEAD]
        key = key * lax.rsqrt(jnp.sum(key * key, axis=-1, keepdims=True) + 1e-06)
        k_ref[j * SEG : (j + 1) * SEG, h * HEAD : (h + 1) * HEAD] = key
        unit.append(key)
        high, low = halves(key)
        dots = mm_t(jnp.concatenate([high, low], 1), jnp.concatenate([high, high], 1)) + mm_t(high, low)
        dcol = decays[j][:, h : h + 1]
        drow = decays[j].T[h : h + 1, :]
        bcol = betas[j][:, HEADS + h : HEADS + h + 1]
        gap = jnp.where(strict, dcol - drow, 0.0)
        lower = jnp.where(strict, bcol * jnp.exp(gap) * dots, 0.0)
        lowers.append(lower)
        blocks += [lower[:HALF, :HALF].astype(bf16), lower[HALF:, HALF:].astype(bf16)]
    values = [mm(tok_ref[j], w_ref[1]) for j in range(LOCAL)]
    diagonal = jnp.where(differ == 0, 1.0, 0.0)
    first = jnp.where(differ == 1, 1.0, 0.0)
    inverses = [diagonal - first * block.astype(f32) for block in blocks]
    step = 2
    while step < HALF:
        mask = jnp.where((differ >= step) & (differ < 2 * step), 1.0, 0.0).astype(bf16)
        narrow = [inverse.astype(bf16) for inverse in inverses]
        inner = [mm(block * mask, thin).astype(bf16) for block, thin in zip(blocks, narrow)]
        inverses = [
            inverse - mm(thin, middle) for inverse, thin, middle in zip(inverses, narrow, inner)
        ]
        step *= 2
    inverses = [inverse.astype(bf16) for inverse in inverses]

    def solve(inverse, lower, right):
        guess = mm(inverse, right.astype(bf16)).astype(bf16)
        rest = right - guess.astype(f32) - wide(lower, guess)
        return guess.astype(f32) + mm(inverse, rest.astype(bf16))

    tops, bottoms = [], []
    for p, (j, h) in enumerate(pairs):
        value = values[j][:, h * HEAD : (h + 1) * HEAD]
        bcol = betas[j][:, HEADS + h : HEADS + h + 1]
        dcol = decays[j][:, h : h + 1]
        rights.append(jnp.concatenate([bcol * value, (bcol * jnp.exp(dcol)) * unit[p]], axis=1))
        tops.append(solve(inverses[2 * p], lowers[p][:HALF, :HALF], rights[p][:HALF]))
    for p in range(len(pairs)):
        high, low = halves(tops[p])
        corner = lowers[p][HALF:, :HALF]
        rest = rights[p][HALF:] - (wide(corner, high) + mm(corner.astype(bf16), low))
        bottoms.append(solve(inverses[2 * p + 1], lowers[p][HALF:, HALF:], rest))
    for p, (j, h) in enumerate(pairs):
        solved = jnp.concatenate([tops[p], bottoms[p]], axis=0)
        x_ref[j, h] = solved.astype(bf16)
        final = decays[j][SEG - 1 : SEG, h : h + 1]
        carried = (jnp.exp(final - decays[j][:, h : h + 1]) * unit[p]).T
        packet_ref[j, h, :HEAD, :] = dot3(carried, solved).astype(bf16)
        overall = jnp.broadcast_to(jnp.exp(final), pack_row.shape)
        high = overall.astype(bf16).astype(f32)
        mid = (overall - high).astype(bf16).astype(f32)
        low = overall - high - mid
        tail = jnp.where(
            pack_row == 0, high, jnp.where(pack_row == 1, mid, jnp.where(pack_row == 2, low, 0.0))
        )
        packet_ref[j, h, HEAD:, :] = tail.astype(bf16)


def local_kernel(tok_ref, w_ref, k_ref, x_ref, d_ref, p_ref, e_ref):
    row = lax.broadcasted_iota(jnp.int32, (SEG, SEG), 0)
    col = lax.broadcasted_iota(jnp.int32, (SEG, SEG), 1)
    for j in range(LOCAL):
        rows = slice(j * SEG, (j + 1) * SEG)
        queries = mm(tok_ref[rows, :], w_ref[0])
        decay = d_ref[rows, :]
        decay_t = decay.T
        for h in range(HEADS):
            cols = slice(h * HEAD, (h + 1) * HEAD)
            query = queries[:, cols]
            query = query * lax.rsqrt(jnp.sum(query * query, axis=-1, keepdims=True) + 1e-06)
            query = query * (1.0 / math.sqrt(HEAD))
            dcol = decay[:, h : h + 1]
            drow = decay_t[h : h + 1, :]
            gap = jnp.where(row >= col, dcol - drow, 0.0)
            mixing = jnp.where(row >= col, jnp.exp(gap) * dot3_t(query, k_ref[rows, cols]), 0.0)
            high, low = halves(mixing)
            both = mm(high, x_ref[j, h]) + mm(low, x_ref[j, h])
            p_ref[rows, cols] = both[:, :HEAD]
            e_ref[rows, cols] = jnp.exp(dcol) * query - both[:, HEAD:]


def slot_of(branch, node):
    device = node // LOCAL
    near = branch - device
    return jnp.where(device // ROW == branch // ROW, near, ROW + (near & (ROW - 1)))


def states_kernel(parents_ref, lengths_ref, p_ref, e_ref, *rest):
    count = parents_ref.shape[0]
    devices = count // LOCAL
    packets = rest[:devices]
    out_ref, pack_ref, ends_ref, flag_ref, sems = rest[devices:]
    branch = lax.axis_index("branch")
    copies = [pltpu.make_async_copy(packets[k], pack_ref.at[k], sems.at[k]) for k in range(devices)]
    for copy in copies:
        copy.start()

    def clear(i, carry):
        flag_ref[i] = 0
        return carry

    lax.fori_loop(0, count, clear, 0)

    def climb(_, current):
        above = parents_ref[current]

        @pl.when(current > 0)
        def _():
            flag_ref[above] = 1

        return above

    for j in range(LOCAL):
        lax.fori_loop(0, count - 1, climb, branch * LOCAL + j)
    for copy in copies:
        copy.wait()

    def advance(node, carry):
        @pl.when(flag_ref[node] > 0)
        def _():
            above = parents_ref[node]
            slot = slot_of(branch, node)
            side = node % LOCAL
            for h in range(HEADS):
                start = jnp.where(node > 0, ends_ref[above, h], 0.0)
                high, low = halves(start)
                packed = pack_ref[slot, side, h]
                linear = packed[:HEAD, HEAD:]
                offset = packed[:HEAD, :HEAD].astype(f32)
                tail = packed[HEAD:, :HEAD].astype(f32)
                overall = tail[0:1, :] + tail[1:2, :] + tail[2:3, :]
                moved = mm(jnp.concatenate([linear, linear], 1), jnp.concatenate([high, low], 0))
                ends_ref[node, h] = overall * start - moved + offset

        return carry

    lax.fori_loop(0, branch * LOCAL + LOCAL - 1, advance, 0)
    for j in range(LOCAL):
        node = branch * LOCAL + j
        above = parents_ref[node]
        rows = slice(j * SEG, (j + 1) * SEG)
        valid = lax.broadcasted_iota(jnp.int32, (SEG, HEAD), 0) < lengths_ref[node]
        for h in range(HEADS):
            cols = slice(h * HEAD, (h + 1) * HEAD)
            start = jnp.where(node > 0, ends_ref[above, h], 0.0)
            heads = p_ref[rows, cols] + dot3_packed(e_ref[rows, cols], start)
            out_ref[rows, cols] = jnp.where(valid, heads, 0.0).astype(bf16)


def mixed_kernel(tok_ref, a_ref, b_ref, c_ref, d_ref, lo_hbm, gain_ref, wkv_ref,
                 mixed_ref, normed_ref, kv_ref, sum_ref, lo_ref, sems):
    tensor = lax.axis_index("tensor")
    width = a_ref.shape[1]
    pieces, _, span = lo_ref.shape
    copies = []
    for n in range(pieces):
        for k in range(4):
            source = pl.multiple_of((tensor ^ k) * width, width)
            copies.append(
                pltpu.make_async_copy(
                    lo_hbm.at[pl.ds(source, width), pl.ds(n * span, span)],
                    lo_ref.at[n, pl.ds(k * width, width)],
                    sems.at[n, k],
                )
            )
            copies[-1].start()
    values = jnp.concatenate([a_ref[...], b_ref[...], c_ref[...], d_ref[...]], axis=1)
    for n in range(pieces):
        for k in range(4):
            copies[4 * n + k].wait()
        cols = slice(n * span, (n + 1) * span)
        sum_ref[:, cols] = tok_ref[:, cols].astype(f32) + mm(values, lo_ref[n])
    for r in range(LOCAL):
        rows = slice(r * SEG, (r + 1) * SEG)
        total = sum_ref[rows, :]
        square = jnp.mean(total * total, axis=-1, keepdims=True)
        normed = (total * lax.rsqrt(square + 1e-06) * gain_ref[...]).astype(bf16)
        normed_ref[rows, :] = normed
        kv_ref[rows, :] = mm(normed, wkv_ref[...]).astype(bf16)
    quarter = mixed_ref.shape[0]
    mixed_ref[...] = sum_ref[pl.ds(pl.multiple_of(tensor * quarter, quarter), quarter), :].astype(bf16)


def self_kernel(lengths_ref, normed_ref, wq_ref, mine_ref, other_ref, q_ref, top_ref, den_ref, acc_ref):
    branch = lax.axis_index("branch")
    first = lax.axis_index("tensor") % 2 == 0
    key_col = lax.broadcasted_iota(jnp.int32, (HEADS * SEG, SEG), 1)
    query_row = lax.broadcasted_iota(jnp.int32, (HEADS * SEG, SEG), 0) & (SEG - 1)
    for j in range(LOCAL):
        rows = slice(j * SEG, (j + 1) * SEG)
        both = mm(normed_ref[rows, :], wq_ref[...]).astype(bf16)
        both = (both.astype(f32) * (1.0 / math.sqrt(ATT_DIM))).astype(bf16)
        queries = jnp.concatenate([both[:, h * ATT_DIM : (h + 1) * ATT_DIM] for h in range(HEADS)], 0)
        q_ref[j] = queries
        mine = mine_ref[rows, :]
        other = other_ref[rows, :]
        keys = jnp.where(first, mine, other)
        values = jnp.where(first, other, mine)
        allowed = (key_col <= query_row) & (key_col < lengths_ref[branch * LOCAL + j])
        scores = jnp.where(allowed, mm_t(queries, keys), NEG)
        top = jnp.max(scores, axis=-1, keepdims=True)
        weights = jnp.exp(scores - top)
        top_ref[j] = jnp.broadcast_to(top, top_ref.shape[1:])
        den_ref[j] = weights[:, :HALF] + weights[:, HALF:]
        acc_ref[j] = mm(weights.astype(bf16), values)


def attend_kernel(parents_ref, lengths_ref, q_ref, top0_ref, den0_ref, acc0_ref, *rest):
    count = parents_ref.shape[0]
    devices = count // LOCAL
    mine = rest[:devices]
    other = rest[devices : 2 * devices]
    out_ref, kv_ref, top_ref, den_ref, acc_ref, list_ref, sems = rest[2 * devices :]
    branch = lax.axis_index("branch")
    core = lax.axis_index("tensor") % 2
    copies = []
    for k in range(devices):
        copies.append(pltpu.make_async_copy(mine[k], kv_ref.at[core, k], sems.at[0, k]))
        copies.append(pltpu.make_async_copy(other[k], kv_ref.at[1 - core, k], sems.at[1, k]))
    for copy in copies:
        copy.start()
    top_ref[...] = top0_ref[...]
    den_ref[...] = den0_ref[...]
    acc_ref[...] = acc0_ref[...]
    query_row = lax.broadcasted_iota(jnp.int32, (SEG, ATT_DIM), 0)
    tile_col = lax.broadcasted_iota(jnp.int32, (1, TILES * HALF), 1)
    lengths = []
    for j in range(LOCAL):

        def climb(_, carry):
            current, found = carry
            above = parents_ref[current]
            more = current > 0

            @pl.when(more)
            def _():
                list_ref[j, found] = 2 * above
                list_ref[j, found + 1] = 2 * above + 1

            size = jnp.where(lengths_ref[above] > HALF, 2, 1)
            return above, found + jnp.where(more, size, 0)

        def clear(i, carry):
            list_ref[j, i] = 0
            return carry

        lax.fori_loop(0, list_ref.shape[1], clear, 0)
        lengths.append(lax.fori_loop(0, count - 1, climb, (branch * LOCAL + j, 0))[1])
    for copy in copies:
        copy.wait()

    def fold(t, carry):
        for j in range(LOCAL):
            keys, values = [], []
            for i in range(TILES):
                entry = list_ref[j, TILES * t + i]
                live = TILES * t + i < lengths[j]
                entry = jnp.where(live, entry, 2 * branch * LOCAL)
                slot = slot_of(branch, entry // 2)
                place = pl.multiple_of((entry % (2 * LOCAL)) * HALF, HALF)
                keys.append(kv_ref[0, slot, pl.ds(place, HALF), :])
                values.append(kv_ref[1, slot, pl.ds(place, HALF), :])
            keys = jnp.concatenate(keys, 0)
            values = jnp.concatenate(values, 0)
            bias = jnp.where(tile_col < (lengths[j] - TILES * t) * HALF, 0.0, NEG)
            for h in range(HEADS):
                rows = slice(h * SEG, (h + 1) * SEG)
                scores = mm_t(q_ref[j, rows, :], keys) + bias
                peak = scores[:, :HALF]
                for i in range(1, TILES):
                    peak = jnp.maximum(peak, scores[:, i * HALF : (i + 1) * HALF])
                old = top_ref[j, rows, :]
                new = jnp.maximum(old, jnp.max(peak, axis=-1, keepdims=True))
                shrink = jnp.exp(old - new)
                weights = jnp.exp(scores - new[:, :1])
                added = weights[:, :HALF]
                for i in range(1, TILES):
                    added = added + weights[:, i * HALF : (i + 1) * HALF]
                top_ref[j, rows, :] = new
                den_ref[j, rows, :] = den_ref[j, rows, :] * shrink + added
                acc_ref[j, rows, :] = acc_ref[j, rows, :] * jnp.concatenate([shrink, shrink], 1) + mm(
                    weights.astype(bf16), values
                )
        return carry

    most = jnp.maximum(lengths[0], lengths[1])
    lax.fori_loop(0, (most + TILES - 1) // TILES, fold, 0)
    for j in range(LOCAL):
        for h in range(HEADS):
            rows = slice(h * SEG, (h + 1) * SEG)
            total = jnp.sum(den_ref[j, rows, :], axis=-1, keepdims=True)
            result = acc_ref[j, rows, :] / total
            result = jnp.where(query_row < lengths_ref[branch * LOCAL + j], result, 0.0)
            out_ref[j * SEG : (j + 1) * SEG, h * ATT_DIM : (h + 1) * ATT_DIM] = result.astype(bf16)


smem = pl.BlockSpec(memory_space=pltpu.SMEM)
vmem = pl.BlockSpec(memory_space=pltpu.VMEM)
anyspace = pl.BlockSpec(memory_space=pl.ANY)


def call(kernel, outs, in_specs, scratch, args, name):
    return pl.pallas_call(
        kernel,
        out_shape=[jax.ShapeDtypeStruct(s, d) for s, d in outs],
        in_specs=in_specs,
        out_specs=[vmem] * len(outs),
        scratch_shapes=scratch,
        compiler_params=pltpu.CompilerParams(vmem_limit_bytes=56 << 20),
        name=name,
    )(*args)


def sibling(piece):
    return lax.ppermute(piece, "tensor", [(0, 1), (1, 0), (2, 3), (3, 2)])


def spread(piece, filler):
    def send(array, pairs):
        return lax.ppermute(array, "branch", pairs)

    ring = range(ROW)
    mirror = send(piece, [(x, ROW + x) for x in ring])
    line = [
        send(piece, [(r + x, r + x + k) for r in (0, ROW) for x in range(ROW - k)]) for k in (1, 2, 3)
    ]
    across = send(piece, [(x, ROW + (x + 2) % ROW) for x in ring])
    mirror, filled = lax.optimization_barrier((mirror, filler()))
    right = send(mirror, [(ROW + x, ROW + (x + 1) % ROW) for x in ring])
    left = send(mirror, [(ROW + x, ROW + (x + 3) % ROW) for x in ring])
    return [piece, *line, mirror, right, across, left], filled


def on_device(
    tokens, parents, lengths, lin_qkv, lin_gates, decay_rate, lin_out, norm_gain, att_q, att_kv
):
    tensor = lax.axis_index("tensor")
    branches = lax.axis_size("branch")
    count = parents.shape[0]
    rows, model_width = tokens.shape
    out_weights = lax.all_gather(lin_out, "tensor", axis=0, tiled=True)
    gates = jnp.transpose(lin_gates, (1, 2, 0))
    weights = jnp.transpose(lin_qkv, (1, 0, 2))
    width = HEADS * HEAD
    packet, k_unit, solved, decay = call(
        maps_kernel,
        [
            ((LOCAL, HEADS, PACK, 2 * HEAD), bf16),
            ((rows, width), f32),
            ((LOCAL, HEADS, SEG, 2 * HEAD), bf16),
            ((rows, 16), f32),
        ],
        [smem, smem, vmem, anyspace, anyspace],
        [
            pltpu.VMEM((LOCAL, SEG, model_width), bf16),
            pltpu.VMEM((2, model_width, width), bf16),
            pltpu.VMEM((16, model_width), bf16),
            pltpu.SemaphoreType.DMA((4,)),
        ],
        (lengths, decay_rate, gates, tokens, weights),
        "branch_maps",
    )
    packets, (base, effect) = spread(
        packet,
        lambda: call(
            local_kernel,
            [((rows, width), f32), ((rows, width), f32)],
            [vmem] * 5,
            [],
            (tokens, weights, k_unit, solved, decay),
            "local_outputs",
        ),
    )
    (lin_values,) = call(
        states_kernel,
        [((rows, width), bf16)],
        [smem, smem, vmem, vmem] + [anyspace] * branches,
        [
            pltpu.VMEM((branches, LOCAL, HEADS, PACK, 2 * HEAD), bf16),
            pltpu.VMEM((count, HEADS, HEAD, HEAD), f32),
            pltpu.SMEM((count,), jnp.int32),
            pltpu.SemaphoreType.DMA((branches,)),
        ],
        (parents, lengths, base, effect, *packets),
        "start_states",
    )
    far = lax.ppermute(lin_values, "tensor", [(i, i ^ 2) for i in range(4)])
    near = sibling(lin_values)
    kv_weights = lax.dynamic_slice(
        att_kv, (0, tensor % 2, (tensor // 2) * ATT_DIM), (model_width, 1, ATT_DIM)
    ).reshape(model_width, ATT_DIM)
    far, kv_weights = lax.optimization_barrier((far, kv_weights))
    parts = [lin_values, near, far, sibling(far)]
    lin_mixed, normed, own_kv = call(
        mixed_kernel,
        [((rows // 4, model_width), bf16), ((rows, model_width), bf16), ((rows, ATT_DIM), bf16)],
        [vmem] * 5 + [anyspace, vmem, vmem],
        [
            pltpu.VMEM((rows, model_width), f32),
            pltpu.VMEM((4, 4 * width, model_width // 4), bf16),
            pltpu.SemaphoreType.DMA((4, 4)),
        ],
        (tokens, *parts, out_weights, norm_gain.reshape(1, -1), kv_weights),
        "mixed_norm",
    )
    state = [
        ((LOCAL, HEADS * SEG, ATT_DIM), bf16),
        ((LOCAL, HEADS * SEG, 128), f32),
        ((LOCAL, HEADS * SEG, 128), f32),
        ((LOCAL, HEADS * SEG, ATT_DIM), f32),
    ]
    own_other = sibling(own_kv)
    mine, begun = spread(
        own_kv,
        lambda: call(
            self_kernel,
            state,
            [smem] + [vmem] * 4,
            [],
            (lengths, normed, att_q, own_kv, own_other),
            "attend_self",
        ),
    )
    other = [own_other] + [sibling(piece) for piece in mine[1:]]
    (att_out,) = call(
        attend_kernel,
        [((rows, att_q.shape[1]), bf16)],
        [smem, smem] + [vmem] * 4 + [anyspace] * (2 * branches),
        [
            pltpu.VMEM((2, branches, rows, ATT_DIM), bf16),
            pltpu.VMEM((LOCAL, HEADS * SEG, 128), f32),
            pltpu.VMEM((LOCAL, HEADS * SEG, 128), f32),
            pltpu.VMEM((LOCAL, HEADS * SEG, ATT_DIM), f32),
            pltpu.SMEM((LOCAL, 2 * count + 2), jnp.int32),
            pltpu.SemaphoreType.DMA((2, branches)),
        ],
        (parents, lengths, *begun, *mine, *other),
        "attend",
    )
    return (lin_mixed, att_out)


def solution(mesh):
    placed = (
        P(("rollout", "branch"), None),
        P("rollout"),
        P("rollout"),
        P(None, None, "tensor"),
        P(None, None, "tensor"),
        P("tensor"),
        P("tensor", None),
        P(),
        P(None, "tensor"),
        P(),
    )
    return jax.shard_map(
        on_device,
        mesh=mesh,
        in_specs=placed,
        out_specs=(P(("rollout", "branch", "tensor"), None), P(("rollout", "branch"), "tensor")),
        check_vma=False,
    )
```

```python
import math

import jax
import jax.numpy as jnp
from jax import lax
from jax.experimental import pallas as pl
from jax.experimental.pallas import tpu as pltpu
from jax.sharding import PartitionSpec as P

KV_HEADS = 2
ATT_DIM = 256
SEG = 256
HALF = 128
HEAD = 128
LOCAL = 2
HEADS = 2
PACK = 528
ROW = 4
TILES = 4
NEG = -1e30

f32 = jnp.float32
bf16 = jnp.bfloat16


def halves(x):
    high = x.astype(bf16)
    return high, (x - high.astype(f32)).astype(bf16)


def mm(a, b):
    return jnp.dot(a, b, preferred_element_type=f32)


def mm_t(a, b):
    return lax.dot_general(a, b, (((1,), (1,)), ((), ())), preferred_element_type=f32)


def dot3(a, b):
    ah, al = halves(a)
    bh, bl = halves(b)
    return mm(ah, bh) + (mm(ah, bl) + mm(al, bh))


def dot3_packed(a, b):
    ah, al = halves(a)
    bh, bl = halves(b)
    return mm(jnp.concatenate([ah, al], 1), jnp.concatenate([bh, bh], 0)) + mm(ah, bl)


def dot3_t(a, b):
    ah, al = halves(a)
    bh, bl = halves(b)
    return mm_t(ah, bh) + (mm_t(ah, bl) + mm_t(al, bh))


def running_sum(x):
    rows = lax.broadcasted_iota(jnp.int32, x.shape, 0)
    step = 1
    while step < x.shape[0]:
        x = x + jnp.where(rows >= step, pltpu.roll(x, step, 0), 0.0)
        step *= 2
    return x


def wide(a, b):
    high, low = halves(a)
    return mm(jnp.concatenate([high, low], 1), jnp.concatenate([b, b], 0))


def maps_kernel(len_ref, rate_ref, gate_in, tok_hbm, w_hbm, packet_ref, k_ref, x_ref, d_ref,
                tok_ref, w_ref, gate_ref, sems):
    branch = lax.axis_index("branch")
    width = HEADS * HEAD
    pairs = [(j, h) for j in range(LOCAL) for h in range(HEADS)]
    loads = [
        pltpu.make_async_copy(w_hbm.at[1], w_ref.at[0], sems.at[0]),
        pltpu.make_async_copy(tok_hbm.at[pl.ds(0, SEG)], tok_ref.at[0], sems.at[1]),
        pltpu.make_async_copy(tok_hbm.at[pl.ds(SEG, SEG)], tok_ref.at[1], sems.at[2]),
        pltpu.make_async_copy(w_hbm.at[2], w_ref.at[1], sems.at[3]),
    ]
    for load in loads:
        load.start()
    gate_ref[...] = jnp.zeros(gate_ref.shape, bf16)
    for c in range(2):
        gate_ref[c * HEADS : (c + 1) * HEADS, :] = gate_in[c]
    lane = lax.broadcasted_iota(jnp.int32, (1, 16), 1)
    rate = jnp.where(lane == 0, rate_ref[0], jnp.where(lane == 1, rate_ref[1], 0.0))
    row = lax.broadcasted_iota(jnp.int32, (SEG, SEG), 0)
    col = lax.broadcasted_iota(jnp.int32, (SEG, SEG), 1)
    gate_row = lax.broadcasted_iota(jnp.int32, (SEG, 16), 0)
    pack_row = lax.broadcasted_iota(jnp.int32, (16, SEG), 0)
    strict = row > col
    differ = row[:HALF, :HALF] ^ col[:HALF, :HALF]
    loads[0].wait()
    keys, decays, betas = [], [], []
    for j in range(LOCAL):
        loads[1 + j].wait()
        keys.append(mm(tok_ref[j], w_ref[0]))
        gates = mm_t(tok_ref[j], gate_ref[...])
        valid = gate_row < len_ref[branch * LOCAL + j]
        betas.append(jnp.where(valid, 1.0 / (1.0 + jnp.exp(-gates)), 0.0))
        soft = jnp.maximum(gates, 0.0) + jnp.log1p(jnp.exp(-jnp.abs(gates)))
        decays.append(running_sum(jnp.where(valid, -rate * soft, 0.0)))
        d_ref[j * SEG : (j + 1) * SEG, :] = decays[j]
    loads[3].wait()
    unit, lowers, rights, blocks = [], [], [], []
    for j, h in pairs:
        key = keys[j][:, h * HEAD : (h + 1) * HEAD]
        key = key * lax.rsqrt(jnp.sum(key * key, axis=-1, keepdims=True) + 1e-06)
        k_ref[j * SEG : (j + 1) * SEG, h * HEAD : (h + 1) * HEAD] = key
        unit.append(key)
        high, low = halves(key)
        dots = mm_t(jnp.concatenate([high, low], 1), jnp.concatenate([high, high], 1)) + mm_t(high, low)
        dcol = decays[j][:, h : h + 1]
        drow = decays[j].T[h : h + 1, :]
        bcol = betas[j][:, HEADS + h : HEADS + h + 1]
        gap = jnp.where(strict, dcol - drow, 0.0)
        lower = jnp.where(strict, bcol * jnp.exp(gap) * dots, 0.0)
        lowers.append(lower)
        blocks += [lower[:HALF, :HALF].astype(bf16), lower[HALF:, HALF:].astype(bf16)]
    values = [mm(tok_ref[j], w_ref[1]) for j in range(LOCAL)]
    diagonal = jnp.where(differ == 0, 1.0, 0.0)
    first = jnp.where(differ == 1, 1.0, 0.0)
    inverses = [diagonal - first * block.astype(f32) for block in blocks]
    step = 2
    while step < HALF:
        mask = jnp.where((differ >= step) & (differ < 2 * step), 1.0, 0.0).astype(bf16)
        narrow = [inverse.astype(bf16) for inverse in inverses]
        inner = [mm(block * mask, thin).astype(bf16) for block, thin in zip(blocks, narrow)]
        inverses = [
            inverse - mm(thin, middle) for inverse, thin, middle in zip(inverses, narrow, inner)
        ]
        step *= 2
    inverses = [inverse.astype(bf16) for inverse in inverses]

    def solve(inverse, lower, right):
        guess = mm(inverse, right.astype(bf16)).astype(bf16)
        rest = right - guess.astype(f32) - wide(lower, guess)
        return guess.astype(f32) + mm(inverse, rest.astype(bf16))

    tops, bottoms = [], []
    for p, (j, h) in enumerate(pairs):
        value = values[j][:, h * HEAD : (h + 1) * HEAD]
        bcol = betas[j][:, HEADS + h : HEADS + h + 1]
        dcol = decays[j][:, h : h + 1]
        rights.append(jnp.concatenate([bcol * value, (bcol * jnp.exp(dcol)) * unit[p]], axis=1))
        tops.append(solve(inverses[2 * p], lowers[p][:HALF, :HALF], rights[p][:HALF]))
    for p in range(len(pairs)):
        high, low = halves(tops[p])
        corner = lowers[p][HALF:, :HALF]
        rest = rights[p][HALF:] - (wide(corner, high) + mm(corner.astype(bf16), low))
        bottoms.append(solve(inverses[2 * p + 1], lowers[p][HALF:, HALF:], rest))
    tail = jnp.zeros(pack_row.shape, f32)
    for p, (j, h) in enumerate(pairs):
        solved = jnp.concatenate([tops[p], bottoms[p]], axis=0)
        x_ref[j, h] = solved.astype(bf16)
        final = decays[j][SEG - 1 : SEG, h : h + 1]
        carried = (jnp.exp(final - decays[j][:, h : h + 1]) * unit[p]).T
        packet_ref[p * HEAD : (p + 1) * HEAD, :] = dot3(carried, solved).astype(bf16)
        overall = jnp.broadcast_to(jnp.exp(final), pack_row.shape)
        high = overall.astype(bf16).astype(f32)
        mid = (overall - high).astype(bf16).astype(f32)
        for i, part in enumerate((high, mid, overall - high - mid)):
            tail = jnp.where(pack_row == 3 * p + i, part, tail)
    packet_ref[len(pairs) * HEAD :, :] = tail.astype(bf16)


def local_kernel(tok_ref, w_ref, k_ref, x_ref, d_ref, p_ref, e_ref):
    row = lax.broadcasted_iota(jnp.int32, (SEG, SEG), 0)
    col = lax.broadcasted_iota(jnp.int32, (SEG, SEG), 1)
    for j in range(LOCAL):
        rows = slice(j * SEG, (j + 1) * SEG)
        queries = mm(tok_ref[rows, :], w_ref[0])
        decay = d_ref[rows, :]
        decay_t = decay.T
        for h in range(HEADS):
            cols = slice(h * HEAD, (h + 1) * HEAD)
            query = queries[:, cols]
            query = query * lax.rsqrt(jnp.sum(query * query, axis=-1, keepdims=True) + 1e-06)
            query = query * (1.0 / math.sqrt(HEAD))
            dcol = decay[:, h : h + 1]
            drow = decay_t[h : h + 1, :]
            gap = jnp.where(row >= col, dcol - drow, 0.0)
            mixing = jnp.where(row >= col, jnp.exp(gap) * dot3_t(query, k_ref[rows, cols]), 0.0)
            high, low = halves(mixing)
            both = mm(high, x_ref[j, h]) + mm(low, x_ref[j, h])
            p_ref[rows, cols] = both[:, :HEAD]
            e_ref[rows, cols] = jnp.exp(dcol) * query - both[:, HEAD:]


def slot_of(branch, node):
    device = node // LOCAL
    near = branch - device
    return jnp.where(device // ROW == branch // ROW, near, ROW + (near & (ROW - 1)))


def states_kernel(parents_ref, lengths_ref, p_ref, e_ref, *rest):
    count = parents_ref.shape[0]
    devices = count // LOCAL
    packets = rest[:devices]
    out_ref, pack_ref, ends_ref, flag_ref, sems = rest[devices:]
    branch = lax.axis_index("branch")
    copies = [pltpu.make_async_copy(packets[k], pack_ref.at[k], sems.at[k]) for k in range(devices)]
    for copy in copies:
        copy.start()

    def clear(i, carry):
        flag_ref[i] = 0
        return carry

    lax.fori_loop(0, count, clear, 0)

    def climb(_, current):
        above = parents_ref[current]

        @pl.when(current > 0)
        def _():
            flag_ref[above] = 1

        return above

    for j in range(LOCAL):
        lax.fori_loop(0, count - 1, climb, branch * LOCAL + j)
    for copy in copies:
        copy.wait()

    tail_row = lax.broadcasted_iota(jnp.int32, (16, HEAD), 0)

    def advance(node, carry):
        @pl.when(flag_ref[node] > 0)
        def _():
            above = parents_ref[node]
            slot = slot_of(branch, node)
            side = node % LOCAL
            for h in range(HEADS):
                start = jnp.where(node > 0, ends_ref[above, h], 0.0)
                high, low = halves(start)
                place = pl.multiple_of((side * HEADS + h) * HEAD, HEAD)
                linear = pack_ref[slot, pl.ds(place, HEAD), HEAD:]
                offset = pack_ref[slot, pl.ds(place, HEAD), :HEAD].astype(f32)
                mine = (tail_row // 3) == side * HEADS + h
                tail = pack_ref[slot, PACK - 16 :, :HEAD].astype(f32)
                overall = jnp.sum(jnp.where(mine, tail, 0.0), axis=0, keepdims=True)
                moved = mm(jnp.concatenate([linear, linear], 1), jnp.concatenate([high, low], 0))
                ends_ref[node, h] = overall * start - moved + offset

        return carry

    lax.fori_loop(0, branch * LOCAL + LOCAL - 1, advance, 0)
    for j in range(LOCAL):
        node = branch * LOCAL + j
        above = parents_ref[node]
        rows = slice(j * SEG, (j + 1) * SEG)
        valid = lax.broadcasted_iota(jnp.int32, (SEG, HEAD), 0) < lengths_ref[node]
        for h in range(HEADS):
            cols = slice(h * HEAD, (h + 1) * HEAD)
            start = jnp.where(node > 0, ends_ref[above, h], 0.0)
            heads = p_ref[rows, cols] + dot3_packed(e_ref[rows, cols], start)
            out_ref[rows, cols] = jnp.where(valid, heads, 0.0).astype(bf16)


def mixed_kernel(tok_ref, a_ref, b_ref, c_ref, d_ref, gain_ref, wkv_ref, l0, l1, l2, l3,
                 mixed_ref, normed_ref, kv_ref, sum_ref, lo_ref, sems):
    tensor = lax.axis_index("tensor")
    pieces, _, span = lo_ref.shape
    copies = []
    for n in range(pieces):
        group, place = [], 0
        for i, source in enumerate((l0, l1, l2, l3)):
            size = source.shape[0]
            group.append(
                pltpu.make_async_copy(
                    source.at[:, pl.ds(n * span, span)],
                    lo_ref.at[n, pl.ds(place, size)],
                    sems.at[n, i],
                )
            )
            group[-1].start()
            place += size
        copies.append(group)
    values = jnp.concatenate([a_ref[...], b_ref[...], c_ref[...], d_ref[...]], axis=1)
    for n in range(pieces):
        for copy in copies[n]:
            copy.wait()
        cols = slice(n * span, (n + 1) * span)
        sum_ref[:, cols] = tok_ref[:, cols].astype(f32) + mm(values, lo_ref[n])
    for r in range(LOCAL):
        rows = slice(r * SEG, (r + 1) * SEG)
        total = sum_ref[rows, :]
        square = jnp.mean(total * total, axis=-1, keepdims=True)
        normed = (total * lax.rsqrt(square + 1e-06) * gain_ref[...]).astype(bf16)
        normed_ref[rows, :] = normed
        kv_ref[rows, :] = mm(normed, wkv_ref[...]).astype(bf16)
    quarter = mixed_ref.shape[0]
    mixed_ref[...] = sum_ref[pl.ds(pl.multiple_of(tensor * quarter, quarter), quarter), :].astype(bf16)


def self_kernel(lengths_ref, normed_ref, wq_ref, mine_ref, other_ref, q_ref, top_ref, den_ref, acc_ref):
    branch = lax.axis_index("branch")
    first = lax.axis_index("tensor") % 2 == 0
    key_col = lax.broadcasted_iota(jnp.int32, (HEADS * SEG, SEG), 1)
    query_row = lax.broadcasted_iota(jnp.int32, (HEADS * SEG, SEG), 0) & (SEG - 1)
    for j in range(LOCAL):
        rows = slice(j * SEG, (j + 1) * SEG)
        both = mm(normed_ref[rows, :], wq_ref[...]).astype(bf16)
        both = (both.astype(f32) * (1.0 / math.sqrt(ATT_DIM))).astype(bf16)
        queries = jnp.concatenate([both[:, h * ATT_DIM : (h + 1) * ATT_DIM] for h in range(HEADS)], 0)
        q_ref[j] = queries
        mine = mine_ref[rows, :]
        other = other_ref[rows, :]
        keys = jnp.where(first, mine, other)
        values = jnp.where(first, other, mine)
        allowed = (key_col <= query_row) & (key_col < lengths_ref[branch * LOCAL + j])
        scores = jnp.where(allowed, mm_t(queries, keys), NEG)
        top = jnp.max(scores, axis=-1, keepdims=True)
        weights = jnp.exp(scores - top)
        top_ref[j] = jnp.broadcast_to(top, top_ref.shape[1:])
        den_ref[j] = weights[:, :HALF] + weights[:, HALF:]
        acc_ref[j] = mm(weights.astype(bf16), values)


def attend_kernel(parents_ref, lengths_ref, q_ref, top0_ref, den0_ref, acc0_ref, *rest):
    count = parents_ref.shape[0]
    devices = count // LOCAL
    mine = rest[:devices]
    other = rest[devices : 2 * devices]
    out_ref, kv_ref, top_ref, den_ref, acc_ref, list_ref, sems = rest[2 * devices :]
    branch = lax.axis_index("branch")
    core = lax.axis_index("tensor") % 2
    copies = []
    for k in range(devices):
        copies.append(pltpu.make_async_copy(mine[k], kv_ref.at[core, k], sems.at[0, k]))
        copies.append(pltpu.make_async_copy(other[k], kv_ref.at[1 - core, k], sems.at[1, k]))
    for copy in copies:
        copy.start()
    top_ref[...] = top0_ref[...]
    den_ref[...] = den0_ref[...]
    acc_ref[...] = acc0_ref[...]
    query_row = lax.broadcasted_iota(jnp.int32, (SEG, ATT_DIM), 0)
    tile_col = lax.broadcasted_iota(jnp.int32, (1, TILES * HALF), 1)
    lengths = []
    for j in range(LOCAL):

        def climb(_, carry):
            current, found = carry
            above = parents_ref[current]
            more = current > 0

            @pl.when(more)
            def _():
                list_ref[j, found] = 2 * above
                list_ref[j, found + 1] = 2 * above + 1

            size = jnp.where(lengths_ref[above] > HALF, 2, 1)
            return above, found + jnp.where(more, size, 0)

        def clear(i, carry):
            list_ref[j, i] = 0
            return carry

        lax.fori_loop(0, list_ref.shape[1], clear, 0)
        lengths.append(lax.fori_loop(0, count - 1, climb, (branch * LOCAL + j, 0))[1])
    for copy in copies:
        copy.wait()

    def fold(t, carry):
        for j in range(LOCAL):
            keys, values = [], []
            for i in range(TILES):
                entry = list_ref[j, TILES * t + i]
                live = TILES * t + i < lengths[j]
                entry = jnp.where(live, entry, 2 * branch * LOCAL)
                slot = slot_of(branch, entry // 2)
                place = pl.multiple_of((entry % (2 * LOCAL)) * HALF, HALF)
                keys.append(kv_ref[0, slot, pl.ds(place, HALF), :])
                values.append(kv_ref[1, slot, pl.ds(place, HALF), :])
            keys = jnp.concatenate(keys, 0)
            values = jnp.concatenate(values, 0)
            bias = jnp.where(tile_col < (lengths[j] - TILES * t) * HALF, 0.0, NEG)
            for h in range(HEADS):
                rows = slice(h * SEG, (h + 1) * SEG)
                scores = mm_t(q_ref[j, rows, :], keys) + bias
                peak = scores[:, :HALF]
                for i in range(1, TILES):
                    peak = jnp.maximum(peak, scores[:, i * HALF : (i + 1) * HALF])
                old = top_ref[j, rows, :]
                new = jnp.maximum(old, jnp.max(peak, axis=-1, keepdims=True))
                shrink = jnp.exp(old - new)
                weights = jnp.exp(scores - new[:, :1])
                added = weights[:, :HALF]
                for i in range(1, TILES):
                    added = added + weights[:, i * HALF : (i + 1) * HALF]
                top_ref[j, rows, :] = new
                den_ref[j, rows, :] = den_ref[j, rows, :] * shrink + added
                acc_ref[j, rows, :] = acc_ref[j, rows, :] * jnp.concatenate([shrink, shrink], 1) + mm(
                    weights.astype(bf16), values
                )
        return carry

    most = jnp.maximum(lengths[0], lengths[1])
    lax.fori_loop(0, (most + TILES - 1) // TILES, fold, 0)
    for j in range(LOCAL):
        for h in range(HEADS):
            rows = slice(h * SEG, (h + 1) * SEG)
            total = jnp.sum(den_ref[j, rows, :], axis=-1, keepdims=True)
            result = acc_ref[j, rows, :] / total
            result = jnp.where(query_row < lengths_ref[branch * LOCAL + j], result, 0.0)
            out_ref[j * SEG : (j + 1) * SEG, h * ATT_DIM : (h + 1) * ATT_DIM] = result.astype(bf16)


smem = pl.BlockSpec(memory_space=pltpu.SMEM)
vmem = pl.BlockSpec(memory_space=pltpu.VMEM)
anyspace = pl.BlockSpec(memory_space=pl.ANY)


def call(kernel, outs, in_specs, scratch, args, name, cost):
    return pl.pallas_call(
        kernel,
        out_shape=[jax.ShapeDtypeStruct(s, d) for s, d in outs],
        in_specs=in_specs,
        out_specs=[vmem] * len(outs),
        scratch_shapes=scratch,
        compiler_params=pltpu.CompilerParams(vmem_limit_bytes=56 << 20),
        cost_estimate=pl.CostEstimate(
            flops=int(cost * 1.1e9), transcendentals=0, bytes_accessed=int(cost * 3.6e6)
        ),
        name=name,
    )(*args)


def distant(piece):
    return lax.ppermute(piece, "tensor", [(i, i ^ 2) for i in range(4)])


def neighbour(piece):
    pairs = [
        (4 * branch + tensor, 4 * (branch ^ ROW) + (tensor ^ 2)) for branch in range(2 * ROW) for tensor in range(4)
    ]
    return lax.ppermute(piece, ("branch", "tensor"), pairs)


def sibling(piece):
    return lax.ppermute(piece, "tensor", [(0, 1), (1, 0), (2, 3), (3, 2)])


def spread(piece, filler, inputs):
    def send(array, pairs):
        return lax.ppermute(array, "branch", pairs)

    ring = range(ROW)
    mirror = send(piece, [(x, ROW + x) for x in ring])
    line = [
        send(piece, [(r + x, r + x + k) for r in (0, ROW) for x in range(ROW - k)]) for k in (1, 2, 3)
    ]
    mirror, again, inputs = lax.optimization_barrier((mirror, piece, inputs))
    right = send(mirror, [(ROW + x, ROW + (x + 1) % ROW) for x in ring])
    left = send(mirror, [(ROW + x, ROW + (x + 3) % ROW) for x in ring])
    across = send(again, [(x, ROW + (x + 2) % ROW) for x in ring])
    filled = filler(*inputs)
    line, filled = lax.optimization_barrier((line, filled))
    return [piece, *line, mirror, right, across, left], filled


def on_device(
    tokens, parents, lengths, lin_qkv, lin_gates, decay_rate, lin_out, norm_gain, att_q, att_kv
):
    tensor = lax.axis_index("tensor")
    branches = lax.axis_size("branch")
    count = parents.shape[0]
    rows, model_width = tokens.shape
    out_near = sibling(lin_out)
    out_far = neighbour(lin_out)
    gates = jnp.transpose(lin_gates, (1, 2, 0))
    weights = jnp.transpose(lin_qkv, (1, 0, 2))
    width = HEADS * HEAD
    packet, k_unit, solved, decay = call(
        maps_kernel,
        [
            ((PACK, 2 * HEAD), bf16),
            ((rows, width), f32),
            ((LOCAL, HEADS, SEG, 2 * HEAD), bf16),
            ((rows, 16), f32),
        ],
        [smem, smem, vmem, anyspace, anyspace],
        [
            pltpu.VMEM((LOCAL, SEG, model_width), bf16),
            pltpu.VMEM((2, model_width, width), bf16),
            pltpu.VMEM((16, model_width), bf16),
            pltpu.SemaphoreType.DMA((4,)),
        ],
        (lengths, decay_rate, gates, tokens, weights),
        "branch_maps", 10,
    )
    packets, (base, effect) = spread(
        packet,
        lambda *inputs: call(
            local_kernel,
            [((rows, width), f32), ((rows, width), f32)],
            [vmem] * 5,
            [],
            inputs[:5],
            "local_outputs",
            7,
        ),
        (tokens, weights, k_unit, solved, decay),
    )
    base, out_far = lax.optimization_barrier((base, out_far))
    out_weights = [lin_out, out_near, out_far, sibling(out_far)]
    (lin_values,) = call(
        states_kernel,
        [((rows, width), bf16)],
        [smem, smem, vmem, vmem] + [anyspace] * branches,
        [
            pltpu.VMEM((branches, PACK, 2 * HEAD), bf16),
            pltpu.VMEM((count, HEADS, HEAD, HEAD), f32),
            pltpu.SMEM((count,), jnp.int32),
            pltpu.SemaphoreType.DMA((branches,)),
        ],
        (parents, lengths, base, effect, *packets),
        "start_states", 7,
    )
    far = distant(lin_values)
    near = sibling(lin_values)
    kv_weights = lax.dynamic_slice(
        att_kv, (0, tensor % 2, (tensor // 2) * ATT_DIM), (model_width, 1, ATT_DIM)
    ).reshape(model_width, ATT_DIM)
    far, kv_weights = lax.optimization_barrier((far, kv_weights))
    parts = [lin_values, near, far, sibling(far)]
    lin_mixed, normed, own_kv = call(
        mixed_kernel,
        [((rows // 4, model_width), bf16), ((rows, model_width), bf16), ((rows, ATT_DIM), bf16)],
        [vmem] * 7 + [anyspace] * 4,
        [
            pltpu.VMEM((rows, model_width), f32),
            pltpu.VMEM((4, 4 * width, model_width // 4), bf16),
            pltpu.SemaphoreType.DMA((4, 4)),
        ],
        (tokens, *parts, norm_gain.reshape(1, -1), kv_weights, *out_weights),
        "mixed_norm", 9,
    )
    state = [
        ((LOCAL, HEADS * SEG, ATT_DIM), bf16),
        ((LOCAL, HEADS * SEG, 128), f32),
        ((LOCAL, HEADS * SEG, 128), f32),
        ((LOCAL, HEADS * SEG, ATT_DIM), f32),
    ]
    own_other = sibling(own_kv)
    mine, begun = spread(
        own_kv,
        lambda *inputs: call(self_kernel, state, [smem] + [vmem] * 4, [], inputs, "attend_self", 6),
        (lengths, normed, att_q, own_kv, own_other),
    )
    other = [own_other] + [sibling(piece) for piece in mine[1:]]
    (att_out,) = call(
        attend_kernel,
        [((rows, att_q.shape[1]), bf16)],
        [smem, smem] + [vmem] * 4 + [anyspace] * (2 * branches),
        [
            pltpu.VMEM((2, branches, rows, ATT_DIM), bf16),
            pltpu.VMEM((LOCAL, HEADS * SEG, 128), f32),
            pltpu.VMEM((LOCAL, HEADS * SEG, 128), f32),
            pltpu.VMEM((LOCAL, HEADS * SEG, ATT_DIM), f32),
            pltpu.SMEM((LOCAL, 2 * count + 2), jnp.int32),
            pltpu.SemaphoreType.DMA((2, branches)),
        ],
        (parents, lengths, *begun, *mine, *other),
        "attend", 12,
    )
    return (lin_mixed, att_out)


def solution(mesh):
    placed = (
        P(("rollout", "branch"), None),
        P("rollout"),
        P("rollout"),
        P(None, None, "tensor"),
        P(None, None, "tensor"),
        P("tensor"),
        P("tensor", None),
        P(),
        P(None, "tensor"),
        P(),
    )
    return jax.shard_map(
        on_device,
        mesh=mesh,
        in_specs=placed,
        out_specs=(P(("rollout", "branch", "tensor"), None), P(("rollout", "branch"), "tensor")),
        check_vma=False,
    )
```

```python
import math

import jax
import jax.numpy as jnp
from jax import lax
from jax.experimental import pallas as pl
from jax.experimental.pallas import tpu as pltpu
from jax.sharding import PartitionSpec as P

KV_HEADS = 2
ATT_DIM = 256
SEG = 256
HALF = 128
HEAD = 128
LOCAL = 2
HEADS = 2
PACK = 528
ROW = 4
TILES = 4
NEG = -1e30

f32 = jnp.float32
bf16 = jnp.bfloat16


def halves(x):
    high = x.astype(bf16)
    return high, (x - high.astype(f32)).astype(bf16)


def mm(a, b):
    return jnp.dot(a, b, preferred_element_type=f32)


def mm_t(a, b):
    return lax.dot_general(a, b, (((1,), (1,)), ((), ())), preferred_element_type=f32)


def dot3(a, b):
    ah, al = halves(a)
    bh, bl = halves(b)
    return mm(ah, bh) + (mm(ah, bl) + mm(al, bh))


def dot3_packed(a, b):
    ah, al = halves(a)
    bh, bl = halves(b)
    return mm(jnp.concatenate([ah, al], 1), jnp.concatenate([bh, bh], 0)) + mm(ah, bl)


def dot3_t(a, b):
    ah, al = halves(a)
    bh, bl = halves(b)
    return mm_t(ah, bh) + (mm_t(ah, bl) + mm_t(al, bh))


def running_sum(x):
    rows = lax.broadcasted_iota(jnp.int32, x.shape, 0)
    step = 1
    while step < x.shape[0]:
        x = x + jnp.where(rows >= step, pltpu.roll(x, step, 0), 0.0)
        step *= 2
    return x


def wide(a, b):
    high, low = halves(a)
    return mm(jnp.concatenate([high, low], 1), jnp.concatenate([b, b], 0))


def maps_kernel(len_ref, rate_ref, gate_in, tok_hbm, w_hbm, packet_ref, k_ref, x_ref, d_ref,
                tok_ref, w_ref, gate_ref, sems):
    branch = lax.axis_index("branch")
    width = HEADS * HEAD
    pairs = [(j, h) for j in range(LOCAL) for h in range(HEADS)]
    loads = [
        pltpu.make_async_copy(w_hbm.at[1], w_ref.at[0], sems.at[0]),
        pltpu.make_async_copy(tok_hbm.at[pl.ds(0, SEG)], tok_ref.at[0], sems.at[1]),
        pltpu.make_async_copy(tok_hbm.at[pl.ds(SEG, SEG)], tok_ref.at[1], sems.at[2]),
        pltpu.make_async_copy(w_hbm.at[2], w_ref.at[1], sems.at[3]),
    ]
    for load in loads:
        load.start()
    gate_ref[...] = jnp.zeros(gate_ref.shape, bf16)
    for c in range(2):
        gate_ref[c * HEADS : (c + 1) * HEADS, :] = gate_in[c]
    lane = lax.broadcasted_iota(jnp.int32, (1, 16), 1)
    rate = jnp.where(lane == 0, rate_ref[0], jnp.where(lane == 1, rate_ref[1], 0.0))
    row = lax.broadcasted_iota(jnp.int32, (SEG, SEG), 0)
    col = lax.broadcasted_iota(jnp.int32, (SEG, SEG), 1)
    gate_row = lax.broadcasted_iota(jnp.int32, (SEG, 16), 0)
    pack_row = lax.broadcasted_iota(jnp.int32, (16, SEG), 0)
    strict = row > col
    differ = row[:HALF, :HALF] ^ col[:HALF, :HALF]
    loads[0].wait()
    keys, decays, betas = [], [], []
    for j in range(LOCAL):
        loads[1 + j].wait()
        keys.append(mm(tok_ref[j], w_ref[0]))
        gates = mm_t(tok_ref[j], gate_ref[...])
        valid = gate_row < len_ref[branch * LOCAL + j]
        betas.append(jnp.where(valid, 1.0 / (1.0 + jnp.exp(-gates)), 0.0))
        soft = jnp.maximum(gates, 0.0) + jnp.log1p(jnp.exp(-jnp.abs(gates)))
        decays.append(running_sum(jnp.where(valid, -rate * soft, 0.0)))
        d_ref[j * SEG : (j + 1) * SEG, :] = decays[j]
    loads[3].wait()
    unit, lowers, rights, blocks = [], [], [], []
    for j, h in pairs:
        key = keys[j][:, h * HEAD : (h + 1) * HEAD]
        key = key * lax.rsqrt(jnp.sum(key * key, axis=-1, keepdims=True) + 1e-06)
        k_ref[j * SEG : (j + 1) * SEG, h * HEAD : (h + 1) * HEAD] = key
        unit.append(key)
        high, low = halves(key)
        dots = mm_t(jnp.concatenate([high, low], 1), jnp.concatenate([high, high], 1)) + mm_t(high, low)
        dcol = decays[j][:, h : h + 1]
        drow = decays[j].T[h : h + 1, :]
        bcol = betas[j][:, HEADS + h : HEADS + h + 1]
        gap = jnp.where(strict, dcol - drow, 0.0)
        lower = jnp.where(strict, bcol * jnp.exp(gap) * dots, 0.0)
        lowers.append(lower)
        blocks += [lower[:HALF, :HALF].astype(bf16), lower[HALF:, HALF:].astype(bf16)]
    values = [mm(tok_ref[j], w_ref[1]) for j in range(LOCAL)]
    diagonal = jnp.where(differ == 0, 1.0, 0.0)
    first = jnp.where(differ == 1, 1.0, 0.0)
    inverses = [diagonal - first * block.astype(f32) for block in blocks]
    step = 2
    while step < HALF:
        mask = jnp.where((differ >= step) & (differ < 2 * step), 1.0, 0.0).astype(bf16)
        narrow = [inverse.astype(bf16) for inverse in inverses]
        inner = [mm(block * mask, thin).astype(bf16) for block, thin in zip(blocks, narrow)]
        inverses = [
            inverse - mm(thin, middle) for inverse, thin, middle in zip(inverses, narrow, inner)
        ]
        step *= 2
    inverses = [inverse.astype(bf16) for inverse in inverses]

    def solve(inverse, lower, right):
        guess = mm(inverse, right.astype(bf16)).astype(bf16)
        rest = right - guess.astype(f32) - wide(lower, guess)
        return guess.astype(f32) + mm(inverse, rest.astype(bf16))

    tops, bottoms = [], []
    for p, (j, h) in enumerate(pairs):
        value = values[j][:, h * HEAD : (h + 1) * HEAD]
        bcol = betas[j][:, HEADS + h : HEADS + h + 1]
        dcol = decays[j][:, h : h + 1]
        rights.append(jnp.concatenate([bcol * value, (bcol * jnp.exp(dcol)) * unit[p]], axis=1))
        tops.append(solve(inverses[2 * p], lowers[p][:HALF, :HALF], rights[p][:HALF]))
    for p in range(len(pairs)):
        high, low = halves(tops[p])
        corner = lowers[p][HALF:, :HALF]
        rest = rights[p][HALF:] - (wide(corner, high) + mm(corner.astype(bf16), low))
        bottoms.append(solve(inverses[2 * p + 1], lowers[p][HALF:, HALF:], rest))
    tail = jnp.zeros(pack_row.shape, f32)
    for p, (j, h) in enumerate(pairs):
        solved = jnp.concatenate([tops[p], bottoms[p]], axis=0)
        x_ref[j, h] = solved.astype(bf16)
        final = decays[j][SEG - 1 : SEG, h : h + 1]
        carried = (jnp.exp(final - decays[j][:, h : h + 1]) * unit[p]).T
        packet_ref[p * HEAD : (p + 1) * HEAD, :] = dot3(carried, solved).astype(bf16)
        overall = jnp.broadcast_to(jnp.exp(final), pack_row.shape)
        high = overall.astype(bf16).astype(f32)
        mid = (overall - high).astype(bf16).astype(f32)
        for i, part in enumerate((high, mid, overall - high - mid)):
            tail = jnp.where(pack_row == 3 * p + i, part, tail)
    packet_ref[len(pairs) * HEAD :, :] = tail.astype(bf16)


def local_kernel(tok_ref, w_ref, k_ref, x_ref, d_ref, p_ref, e_ref):
    row = lax.broadcasted_iota(jnp.int32, (SEG, SEG), 0)
    col = lax.broadcasted_iota(jnp.int32, (SEG, SEG), 1)
    for j in range(LOCAL):
        rows = slice(j * SEG, (j + 1) * SEG)
        queries = mm(tok_ref[rows, :], w_ref[0])
        decay = d_ref[rows, :]
        decay_t = decay.T
        for h in range(HEADS):
            cols = slice(h * HEAD, (h + 1) * HEAD)
            query = queries[:, cols]
            query = query * lax.rsqrt(jnp.sum(query * query, axis=-1, keepdims=True) + 1e-06)
            query = query * (1.0 / math.sqrt(HEAD))
            dcol = decay[:, h : h + 1]
            drow = decay_t[h : h + 1, :]
            gap = jnp.where(row >= col, dcol - drow, 0.0)
            mixing = jnp.where(row >= col, jnp.exp(gap) * dot3_t(query, k_ref[rows, cols]), 0.0)
            high, low = halves(mixing)
            both = mm(high, x_ref[j, h]) + mm(low, x_ref[j, h])
            p_ref[rows, cols] = both[:, :HEAD]
            e_ref[rows, cols] = jnp.exp(dcol) * query - both[:, HEAD:]


def slot_of(branch, node):
    device = node // LOCAL
    near = branch - device
    return jnp.where(device // ROW == branch // ROW, near, ROW + (near & (ROW - 1)))


def states_kernel(parents_ref, lengths_ref, p_ref, e_ref, *rest):
    count = parents_ref.shape[0]
    devices = count // LOCAL
    packets = rest[:devices]
    out_ref, pack_ref, ends_ref, flag_ref, sems = rest[devices:]
    branch = lax.axis_index("branch")
    copies = [pltpu.make_async_copy(packets[k], pack_ref.at[k], sems.at[k]) for k in range(devices)]
    for copy in copies:
        copy.start()

    def clear(i, carry):
        flag_ref[i] = 0
        return carry

    lax.fori_loop(0, count, clear, 0)

    def climb(_, current):
        above = parents_ref[current]

        @pl.when(current > 0)
        def _():
            flag_ref[above] = 1

        return above

    for j in range(LOCAL):
        lax.fori_loop(0, count - 1, climb, branch * LOCAL + j)
    for copy in copies:
        copy.wait()

    tail_row = lax.broadcasted_iota(jnp.int32, (16, HEAD), 0)

    def advance(node, carry):
        @pl.when(flag_ref[node] > 0)
        def _():
            above = parents_ref[node]
            slot = slot_of(branch, node)
            side = node % LOCAL
            for h in range(HEADS):
                start = jnp.where(node > 0, ends_ref[above, h], 0.0)
                high, low = halves(start)
                place = pl.multiple_of((side * HEADS + h) * HEAD, HEAD)
                linear = pack_ref[slot, pl.ds(place, HEAD), HEAD:]
                offset = pack_ref[slot, pl.ds(place, HEAD), :HEAD].astype(f32)
                mine = (tail_row // 3) == side * HEADS + h
                tail = pack_ref[slot, PACK - 16 :, :HEAD].astype(f32)
                overall = jnp.sum(jnp.where(mine, tail, 0.0), axis=0, keepdims=True)
                moved = mm(jnp.concatenate([linear, linear], 1), jnp.concatenate([high, low], 0))
                ends_ref[node, h] = overall * start - moved + offset

        return carry

    lax.fori_loop(0, branch * LOCAL + LOCAL - 1, advance, 0)
    for j in range(LOCAL):
        node = branch * LOCAL + j
        above = parents_ref[node]
        rows = slice(j * SEG, (j + 1) * SEG)
        valid = lax.broadcasted_iota(jnp.int32, (SEG, HEAD), 0) < lengths_ref[node]
        for h in range(HEADS):
            cols = slice(h * HEAD, (h + 1) * HEAD)
            start = jnp.where(node > 0, ends_ref[above, h], 0.0)
            heads = p_ref[rows, cols] + dot3_packed(e_ref[rows, cols], start)
            out_ref[rows, cols] = jnp.where(valid, heads, 0.0).astype(bf16)


def mixed_kernel(a_ref, b_ref, c_ref, d_ref, gain_ref, tok_hbm, wkv_hbm, l0, l1, l2, l3,
                 mixed_ref, normed_ref, kv_ref, sum_ref, lo_ref, tok_ref, wkv_ref, sems):
    tensor = lax.axis_index("tensor")
    pieces, _, span = lo_ref.shape
    copies = []
    for n in range(pieces):
        group, place = [], 0
        for i, source in enumerate((l0, l1, l2, l3)):
            size = source.shape[0]
            group.append(
                pltpu.make_async_copy(
                    source.at[:, pl.ds(n * span, span)],
                    lo_ref.at[n, pl.ds(place, size)],
                    sems.at[n, i],
                )
            )
            group[-1].start()
            place += size
        group.append(
            pltpu.make_async_copy(tok_hbm.at[:, pl.ds(n * span, span)], tok_ref.at[n], sems.at[n, 4])
        )
        group[-1].start()
        copies.append(group)
    load = pltpu.make_async_copy(wkv_hbm, wkv_ref, sems.at[0, 5])
    load.start()
    values = jnp.concatenate([a_ref[...], b_ref[...], c_ref[...], d_ref[...]], axis=1)
    for n in range(pieces):
        for copy in copies[n]:
            copy.wait()
        cols = slice(n * span, (n + 1) * span)
        sum_ref[:, cols] = tok_ref[n].astype(f32) + mm(values, lo_ref[n])
    load.wait()
    for r in range(LOCAL):
        rows = slice(r * SEG, (r + 1) * SEG)
        total = sum_ref[rows, :]
        square = jnp.mean(total * total, axis=-1, keepdims=True)
        normed = (total * lax.rsqrt(square + 1e-06) * gain_ref[...]).astype(bf16)
        normed_ref[rows, :] = normed
        kv_ref[rows, :] = mm(normed, wkv_ref[...]).astype(bf16)
    quarter = mixed_ref.shape[0]
    mixed_ref[...] = sum_ref[pl.ds(pl.multiple_of(tensor * quarter, quarter), quarter), :].astype(bf16)


def self_kernel(lengths_ref, normed_ref, wq_ref, mine_ref, other_ref, q_ref, top_ref, den_ref, acc_ref):
    branch = lax.axis_index("branch")
    first = lax.axis_index("tensor") % 2 == 0
    key_col = lax.broadcasted_iota(jnp.int32, (HEADS * SEG, SEG), 1)
    query_row = lax.broadcasted_iota(jnp.int32, (HEADS * SEG, SEG), 0) & (SEG - 1)
    for j in range(LOCAL):
        rows = slice(j * SEG, (j + 1) * SEG)
        both = mm(normed_ref[rows, :], wq_ref[...]).astype(bf16)
        both = (both.astype(f32) * (1.0 / math.sqrt(ATT_DIM))).astype(bf16)
        queries = jnp.concatenate([both[:, h * ATT_DIM : (h + 1) * ATT_DIM] for h in range(HEADS)], 0)
        q_ref[j] = queries
        mine = mine_ref[rows, :]
        other = other_ref[rows, :]
        keys = jnp.where(first, mine, other)
        values = jnp.where(first, other, mine)
        allowed = (key_col <= query_row) & (key_col < lengths_ref[branch * LOCAL + j])
        scores = jnp.where(allowed, mm_t(queries, keys), NEG)
        top = jnp.max(scores, axis=-1, keepdims=True)
        weights = jnp.exp(scores - top)
        top_ref[j] = jnp.broadcast_to(top, top_ref.shape[1:])
        den_ref[j] = weights[:, :HALF] + weights[:, HALF:]
        acc_ref[j] = mm(weights.astype(bf16), values)


def attend_kernel(parents_ref, lengths_ref, q_ref, top0_ref, den0_ref, acc0_ref, *rest):
    count = parents_ref.shape[0]
    devices = count // LOCAL
    mine = rest[:devices]
    other = rest[devices : 2 * devices]
    out_ref, kv_ref, top_ref, den_ref, acc_ref, list_ref, sems = rest[2 * devices :]
    branch = lax.axis_index("branch")
    core = lax.axis_index("tensor") % 2
    copies = []
    for k in range(devices):
        copies.append(pltpu.make_async_copy(mine[k], kv_ref.at[core, k], sems.at[0, k]))
        copies.append(pltpu.make_async_copy(other[k], kv_ref.at[1 - core, k], sems.at[1, k]))
    for copy in copies:
        copy.start()
    top_ref[...] = top0_ref[...]
    den_ref[...] = den0_ref[...]
    acc_ref[...] = acc0_ref[...]
    query_row = lax.broadcasted_iota(jnp.int32, (SEG, ATT_DIM), 0)
    tile_col = lax.broadcasted_iota(jnp.int32, (1, TILES * HALF), 1)
    lengths = []
    for j in range(LOCAL):

        def climb(_, carry):
            current, found = carry
            above = parents_ref[current]
            more = current > 0

            @pl.when(more)
            def _():
                list_ref[j, found] = 2 * above
                list_ref[j, found + 1] = 2 * above + 1

            size = jnp.where(lengths_ref[above] > HALF, 2, 1)
            return above, found + jnp.where(more, size, 0)

        def clear(i, carry):
            list_ref[j, i] = 0
            return carry

        lax.fori_loop(0, list_ref.shape[1], clear, 0)
        lengths.append(lax.fori_loop(0, count - 1, climb, (branch * LOCAL + j, 0))[1])
    for copy in copies:
        copy.wait()

    def fold(t, carry):
        for j in range(LOCAL):
            keys, values = [], []
            for i in range(TILES):
                entry = list_ref[j, TILES * t + i]
                live = TILES * t + i < lengths[j]
                entry = jnp.where(live, entry, 2 * branch * LOCAL)
                slot = slot_of(branch, entry // 2)
                place = pl.multiple_of((entry % (2 * LOCAL)) * HALF, HALF)
                keys.append(kv_ref[0, slot, pl.ds(place, HALF), :])
                values.append(kv_ref[1, slot, pl.ds(place, HALF), :])
            keys = jnp.concatenate(keys, 0)
            values = jnp.concatenate(values, 0)
            bias = jnp.where(tile_col < (lengths[j] - TILES * t) * HALF, 0.0, NEG)
            for h in range(HEADS):
                rows = slice(h * SEG, (h + 1) * SEG)
                scores = mm_t(q_ref[j, rows, :], keys) + bias
                peak = scores[:, :HALF]
                for i in range(1, TILES):
                    peak = jnp.maximum(peak, scores[:, i * HALF : (i + 1) * HALF])
                old = top_ref[j, rows, :]
                new = jnp.maximum(old, jnp.max(peak, axis=-1, keepdims=True))
                shrink = jnp.exp(old - new)
                weights = jnp.exp(scores - new[:, :1])
                added = weights[:, :HALF]
                for i in range(1, TILES):
                    added = added + weights[:, i * HALF : (i + 1) * HALF]
                top_ref[j, rows, :] = new
                den_ref[j, rows, :] = den_ref[j, rows, :] * shrink + added
                acc_ref[j, rows, :] = acc_ref[j, rows, :] * jnp.concatenate([shrink, shrink], 1) + mm(
                    weights.astype(bf16), values
                )
        return carry

    most = jnp.maximum(lengths[0], lengths[1])
    lax.fori_loop(0, (most + TILES - 1) // TILES, fold, 0)
    for j in range(LOCAL):
        for h in range(HEADS):
            rows = slice(h * SEG, (h + 1) * SEG)
            total = jnp.sum(den_ref[j, rows, :], axis=-1, keepdims=True)
            result = acc_ref[j, rows, :] / total
            result = jnp.where(query_row < lengths_ref[branch * LOCAL + j], result, 0.0)
            out_ref[j * SEG : (j + 1) * SEG, h * ATT_DIM : (h + 1) * ATT_DIM] = result.astype(bf16)


smem = pl.BlockSpec(memory_space=pltpu.SMEM)
vmem = pl.BlockSpec(memory_space=pltpu.VMEM)
anyspace = pl.BlockSpec(memory_space=pl.ANY)


def call(kernel, outs, in_specs, scratch, args, name, cost):
    return pl.pallas_call(
        kernel,
        out_shape=[jax.ShapeDtypeStruct(s, d) for s, d in outs],
        in_specs=in_specs,
        out_specs=[vmem] * len(outs),
        scratch_shapes=scratch,
        compiler_params=pltpu.CompilerParams(vmem_limit_bytes=56 << 20),
        cost_estimate=pl.CostEstimate(
            flops=int(cost * 1.1e9), transcendentals=0, bytes_accessed=int(cost * 3.6e6)
        ),
        name=name,
    )(*args)


def distant(piece):
    return lax.ppermute(piece, "tensor", [(i, i ^ 2) for i in range(4)])


def neighbour(piece):
    pairs = [
        (4 * branch + tensor, 4 * (branch ^ ROW) + (tensor ^ 2)) for branch in range(2 * ROW) for tensor in range(4)
    ]
    return lax.ppermute(piece, ("branch", "tensor"), pairs)


def sibling(piece):
    return lax.ppermute(piece, "tensor", [(0, 1), (1, 0), (2, 3), (3, 2)])


def spread(piece, filler, inputs, last=False):
    def send(array, pairs):
        return lax.ppermute(array, "branch", pairs)

    ring = range(ROW)
    mirror = send(piece, [(x, ROW + x) for x in ring])
    line = [
        send(piece, [(r + x, r + x + k) for r in (0, ROW) for x in range(ROW - k)]) for k in (1, 2, 3)
    ]
    mirror, again, inputs = lax.optimization_barrier((mirror, piece, inputs))
    right = send(mirror, [(ROW + x, ROW + (x + 1) % ROW) for x in ring])
    left = send(mirror, [(ROW + x, ROW + (x + 3) % ROW) for x in ring])
    across = send(again, [(x, ROW + (x + 2) % ROW) for x in ring])
    filled = filler(*inputs)
    if last:
        right, filled = lax.optimization_barrier((right, filled))
    else:
        line, filled = lax.optimization_barrier((line, filled))
    return [piece, *line, mirror, right, across, left], filled


def on_device(
    tokens, parents, lengths, lin_qkv, lin_gates, decay_rate, lin_out, norm_gain, att_q, att_kv
):
    tensor = lax.axis_index("tensor")
    branches = lax.axis_size("branch")
    count = parents.shape[0]
    rows, model_width = tokens.shape
    out_near = sibling(lin_out)
    out_far = neighbour(lin_out)
    gates = jnp.transpose(lin_gates, (1, 2, 0))
    weights = jnp.transpose(lin_qkv, (1, 0, 2))
    width = HEADS * HEAD
    packet, k_unit, solved, decay = call(
        maps_kernel,
        [
            ((PACK, 2 * HEAD), bf16),
            ((rows, width), f32),
            ((LOCAL, HEADS, SEG, 2 * HEAD), bf16),
            ((rows, 16), f32),
        ],
        [smem, smem, vmem, anyspace, anyspace],
        [
            pltpu.VMEM((LOCAL, SEG, model_width), bf16),
            pltpu.VMEM((2, model_width, width), bf16),
            pltpu.VMEM((16, model_width), bf16),
            pltpu.SemaphoreType.DMA((4,)),
        ],
        (lengths, decay_rate, gates, tokens, weights),
        "branch_maps", 10,
    )
    packets, (base, effect) = spread(
        packet,
        lambda *inputs: call(
            local_kernel,
            [((rows, width), f32), ((rows, width), f32)],
            [vmem] * 5,
            [],
            inputs[:5],
            "local_outputs",
            7,
        ),
        (tokens, weights, k_unit, solved, decay),
    )
    base, out_far = lax.optimization_barrier((base, out_far))
    out_weights = [lin_out, out_near, out_far, sibling(out_far)]
    (lin_values,) = call(
        states_kernel,
        [((rows, width), bf16)],
        [smem, smem, vmem, vmem] + [anyspace] * branches,
        [
            pltpu.VMEM((branches, PACK, 2 * HEAD), bf16),
            pltpu.VMEM((count, HEADS, HEAD, HEAD), f32),
            pltpu.SMEM((count,), jnp.int32),
            pltpu.SemaphoreType.DMA((branches,)),
        ],
        (parents, lengths, base, effect, *packets),
        "start_states", 7,
    )
    far = distant(lin_values)
    near = sibling(lin_values)
    kv_weights = lax.dynamic_slice(
        att_kv, (0, tensor % 2, (tensor // 2) * ATT_DIM), (model_width, 1, ATT_DIM)
    ).reshape(model_width, ATT_DIM)
    far, kv_weights = lax.optimization_barrier((far, kv_weights))
    parts = [lin_values, near, far, sibling(far)]
    lin_mixed, normed, own_kv = call(
        mixed_kernel,
        [((rows // 4, model_width), bf16), ((rows, model_width), bf16), ((rows, ATT_DIM), bf16)],
        [vmem] * 5 + [anyspace] * 6,
        [
            pltpu.VMEM((rows, model_width), f32),
            pltpu.VMEM((4, 4 * width, model_width // 4), bf16),
            pltpu.VMEM((4, rows, model_width // 4), bf16),
            pltpu.VMEM((model_width, ATT_DIM), bf16),
            pltpu.SemaphoreType.DMA((4, 6)),
        ],
        (*parts, norm_gain.reshape(1, -1), tokens, kv_weights, *out_weights),
        "mixed_norm", 9,
    )
    state = [
        ((LOCAL, HEADS * SEG, ATT_DIM), bf16),
        ((LOCAL, HEADS * SEG, 128), f32),
        ((LOCAL, HEADS * SEG, 128), f32),
        ((LOCAL, HEADS * SEG, ATT_DIM), f32),
    ]
    own_other = sibling(own_kv)
    mine, begun = spread(
        own_kv,
        lambda *inputs: call(self_kernel, state, [smem] + [vmem] * 4, [], inputs, "attend_self", 6),
        (lengths, normed, att_q, own_kv, own_other),
        last=True,
    )
    other = [own_other] + [sibling(piece) for piece in mine[1:]]
    (att_out,) = call(
        attend_kernel,
        [((rows, att_q.shape[1]), bf16)],
        [smem, smem] + [vmem] * 4 + [anyspace] * (2 * branches),
        [
            pltpu.VMEM((2, branches, rows, ATT_DIM), bf16),
            pltpu.VMEM((LOCAL, HEADS * SEG, 128), f32),
            pltpu.VMEM((LOCAL, HEADS * SEG, 128), f32),
            pltpu.VMEM((LOCAL, HEADS * SEG, ATT_DIM), f32),
            pltpu.SMEM((LOCAL, 2 * count + 2), jnp.int32),
            pltpu.SemaphoreType.DMA((2, branches)),
        ],
        (parents, lengths, *begun, *mine, *other),
        "attend", 12,
    )
    return (lin_mixed, att_out)


def solution(mesh):
    placed = (
        P(("rollout", "branch"), None),
        P("rollout"),
        P("rollout"),
        P(None, None, "tensor"),
        P(None, None, "tensor"),
        P("tensor"),
        P("tensor", None),
        P(),
        P(None, "tensor"),
        P(),
    )
    return jax.shard_map(
        on_device,
        mesh=mesh,
        in_specs=placed,
        out_specs=(P(("rollout", "branch", "tensor"), None), P(("rollout", "branch"), "tensor")),
        check_vma=False,
    )
```
